512 devices in a mesh: dp: 2 (over y_lo), row: 8 (over y_hi, core), col: 32 (over z, x).
Axes of the slice: x: 4, y: 8 (y_hi: 4, y_lo: 2; y = y_hi * 2 + y_lo), z: 8, core: 2. Of those that a mesh axis runs over, the one named last changes fastest.
Arguments:
- gate_pre: bfloat16 [2048, 28672], P(('dp', 'row'), 'col'), may hold values from -6 to 6
- up_pre: bfloat16 [2048, 28672], P(('dp', 'row'), 'col'), may hold values from -6 to 6
- grad_out: bfloat16 [2048, 16384], P('col', ('dp', 'row')), may hold values from -6 to 6
- down_weight: bfloat16 [28672, 16384], P('col', ('dp', 'row')), may hold values from -0.046875 to 0.046875
- basis: bfloat16 [512, 28672], P(('dp', 'row'), 'col'), may hold values from -0.0625 to 0.0625
- first_moment_in: float32 [512, 16384], P('col', ('dp', 'row')), may hold values from -6 to 6
- second_moment_in: float32 [512, 16384], P('col', ('dp', 'row')), may hold values from 0.1 to 10
Outputs:
- grad_gate: bfloat16 [2048, 28672], P(('dp', 'row'), 'col')
- grad_up: bfloat16 [2048, 28672], P(('dp', 'row'), 'col')
- scaled_grad: bfloat16 [28672, 16384], P('col', ('dp', 'row'))
- first_moment: float32 [512, 16384], P('col', ('dp', 'row'))
- second_moment: float32 [512, 16384], P('col', ('dp', 'row'))
The draws below stay inside these ranges and needn't reach their ends.
All inputs are finite; a program needn't handle non-finite values.
Results may differ from the reference program's by a relative error of at most 0.024.
Values may be sent and summed in bfloat16 or wider, within the bound.
No kernel may reach another device: no remote copies, remote signals or barrier semaphores. Data moves between devices by JAX's collectives and lax.ppermute only.
A program may use at most 64 MiB of HBM per device.

```python
import math
import jax
import jax.numpy as jnp
from jax import lax

D = 16384
FF = 28672
RANK = 512
TOKENS = 2048
N_DP = 2
N_ROW = 8


def raised(drawn, stream_key, source, target, blocks, factor):
    def block_of(position):
        return (jnp.arange(drawn.shape[position]) // (drawn.shape[position] // blocks)).reshape((-1,) + (1,) * (drawn.ndim - 1 - position))

    first = jax.random.permutation(stream_key, blocks)[block_of(target)]
    other_side = (block_of(target) + blocks // 2) % blocks
    return jnp.where((block_of(source) == first) | (block_of(source) == other_side), factor * drawn, drawn)


def steps_of(stream_key, extent, split, smallest, largest):
    factor_of, own = 1.0, jax.random.fold_in(stream_key, 6)
    for dim, blocks in split:
        steps = jnp.exp(jax.random.uniform(jax.random.fold_in(own, dim), (blocks,), jnp.float32, smallest / len(split), largest / len(split)))
        factor_of = factor_of * jnp.repeat(steps, extent[dim] // blocks).reshape([-1 if axis == dim else 1 for axis in range(len(extent))])
    return factor_of


def noise(rng, dims, scale, bound, cuts=(), held_as=jnp.bfloat16):
    array = scale * jax.random.normal(rng, dims, jnp.float32)
    if cuts:
        array = array * steps_of(rng, dims, cuts, -0.22, 0.18)
    return jnp.clip(array, -bound, bound).astype(held_as)


def gaussian_with(key, extent, width, limit, pieces, heavy, kind=jnp.bfloat16):
    values = width * jax.random.normal(key, extent, jnp.float32)
    if pieces:
        values = values * steps_of(key, extent, pieces, -0.22, 0.18)
    return jnp.clip(raised(values, jax.random.fold_in(key, 3), *heavy), -limit, limit).astype(kind)


def setup_inputs(seed: int = 0) -> dict:
    splits = jax.random.split(jax.random.key(seed), 8)
    return {
        "gate_pre": noise(splits[0], (TOKENS, FF), 1.0, 6.0, ((0, 16), (1, 32))),
        "up_pre": noise(splits[1], (TOKENS, FF), 1.0, 6.0, ((0, 16), (1, 32))),
        "grad_out": gaussian_with(splits[2], (TOKENS, D), 1.0, 6.0, ((0, 32), (1, 16)), (1, 0, 32, 2.75)),
        "down_weight": noise(splits[3], (FF, D), D ** -0.5, 0.046875, ((0, 32), (1, 16))),
        "basis": gaussian_with(splits[4], (RANK, FF), FF ** -0.5, 0.0625, ((0, 16), (1, 32)), (1, 0, 32, 2.75)),
        "first_moment_in": noise(splits[5], (RANK, D), 1.0, 6.0, ((0, 32), (1, 16)), jnp.float32),
        "second_moment_in": jnp.clip(jnp.exp(math.log(10.0) - 4.6051702 * jax.random.uniform(splits[6], (RANK, D), jnp.float32) ** steps_of(splits[6], (RANK, D), ((0, 32), (1, 16)), -0.2, 0.2)), 0.1, 10.0),
    }


first_fix = 1.0 - math.exp(1000.0 * math.log(0.9))
second_fix = 1.0 - math.exp(1000.0 * math.log(0.999))

def reference(gate_pre, up_pre, grad_out, down_weight, basis, first_moment_in, second_moment_in):
    gate_f = gate_pre.astype(jnp.float32)
    up_f = up_pre.astype(jnp.float32)
    sigma = jax.nn.sigmoid(gate_f)
    act_value = gate_f * sigma
    hidden = (act_value * up_f).astype(jnp.bfloat16)
    block_count = N_DP * N_ROW
    block_width = D // block_count
    out_blocks = grad_out.reshape(TOKENS, block_count, block_width)
    weight_blocks = down_weight.reshape(FF, block_count, block_width)

    def add_block(block_idx, running):
        out_part = lax.dynamic_index_in_dim(out_blocks, block_idx, 1, keepdims=False)
        weight_part = lax.dynamic_index_in_dim(weight_blocks, block_idx, 1, keepdims=False)
        partial_term = lax.dot_general(out_part, weight_part, (((1,), (1,)), ((), ())), preferred_element_type=jnp.float32)
        rounded = lax.optimization_barrier(partial_term.astype(jnp.bfloat16))
        return running + rounded.astype(jnp.float32)
    summed = lax.fori_loop(0, block_count, add_block, jnp.zeros((TOKENS, FF), jnp.float32))
    grad_hidden = lax.optimization_barrier(summed.astype(jnp.bfloat16)).astype(jnp.float32)
    grad_up = (grad_hidden * act_value).astype(jnp.bfloat16)
    grad_gate = (grad_hidden * up_f * sigma * (1.0 + gate_f * (1.0 - sigma))).astype(jnp.bfloat16)
    grad_weight = lax.dot_general(hidden, grad_out, (((0,), (0,)), ((), ())), preferred_element_type=jnp.float32).astype(jnp.bfloat16)
    token_proj = lax.dot_general(basis, hidden, (((1,), (1,)), ((), ())), preferred_element_type=jnp.float32)
    projected = jnp.dot(token_proj, grad_out.astype(jnp.float32), precision=lax.Precision.HIGHEST)
    first_moment = 0.9 * first_moment_in + 0.1 * projected
    second_moment = 0.999 * second_moment_in + 0.001 * projected * projected
    adapted = first_moment / first_fix / (jnp.sqrt(second_moment / second_fix) + 1e-06)
    column_scale = jnp.sqrt(lax.optimization_barrier(jnp.sum(adapted * adapted, axis=0))) / (jnp.sqrt(lax.optimization_barrier(jnp.sum(projected * projected, axis=0))) + 1e-06)
    scaled_grad = (grad_weight.astype(jnp.float32) * column_scale[None, :]).astype(jnp.bfloat16)
    return (grad_gate, grad_up, scaled_grad, first_moment, second_moment)
```

```python
import math

import jax
import jax.numpy as jnp
from jax import lax
from jax.experimental import pallas as pl
from jax.experimental.pallas import tpu as pltpu
from jax.sharding import PartitionSpec as P


first_fix = 1.0 - math.exp(1000.0 * math.log(0.9))
second_fix = 1.0 - math.exp(1000.0 * math.log(0.999))

BF = jnp.bfloat16
F32 = jnp.float32
TOK = ("dp", "row")
Z_GROUPS = [[4 * z + x for z in range(8)] for x in range(4)]
Y_GROUPS = [[2 * m + q for m in range(8)] for q in range(2)]
PAIR = [(k, k ^ 1) for k in range(16)]
CHUNKS = ((0, 24), (24, 64))


def along_x(value, step):
    return lax.ppermute(value, "col", [(c, c - c % 4 + (c % 4 + step) % 4) for c in range(32)])


def activation(gate_pre, up_pre):
    gate_f = gate_pre.astype(F32)
    sigma = jax.nn.sigmoid(gate_f)
    return gate_f, sigma, gate_f * sigma, up_pre.astype(F32)


def dot_nt(left, right):
    return lax.dot_general(left, right, (((1,), (1,)), ((), ())), preferred_element_type=F32)


def dot_tn(left, right):
    return lax.dot_general(left, right, (((0,), (0,)), ((), ())), preferred_element_type=F32)


def place_kernel(x_ref, here, left, right, far_low, far_high, out, sems):
    x = x_ref[0]
    half = far_low.shape[0]
    copies = []
    for piece, back, rows in (
        (here, 0, None),
        (left, 1, None),
        (right, 3, None),
        (far_low, 2, pl.ds(0, half)),
        (far_high, 2, pl.ds(half, half)),
    ):
        source = lax.rem(x + 4 - back, 4)
        target = out.at[:, source] if rows is None else out.at[rows, source]
        copies.append(pltpu.make_async_copy(piece, target, sems.at[len(copies)]))
    for copy in copies:
        copy.start()
    for copy in copies:
        copy.wait()


def place(x, pieces):
    planes, rows, width = pieces[0].shape
    return pl.pallas_call(
        place_kernel,
        out_shape=jax.ShapeDtypeStruct((planes, 4, rows, width), pieces[0].dtype),
        in_specs=[pl.BlockSpec(memory_space=pltpu.SMEM)] + [pl.BlockSpec(memory_space=pl.ANY)] * 5,
        out_specs=pl.BlockSpec(memory_space=pl.ANY),
        scratch_shapes=[pltpu.SemaphoreType.DMA((5,))],
        name="place",
    )(x[None], *pieces)


def gather_rows(value, x):
    sent = jnp.broadcast_to(value[None], (8,) + value.shape).reshape((-1,) + value.shape[1:])
    here = lax.all_to_all(sent, "col", 0, 0, tiled=True, axis_index_groups=Z_GROUPS)
    here = here.reshape((8,) + value.shape)
    left = along_x(here, 1)
    right = along_x(here, -1)
    far_low = along_x(left[:4], 1)
    far_high = along_x(right[4:], -1)
    return place(x, (here, left, right, far_low, far_high))


def exact(left, right):
    high = left.astype(BF)
    rest = left - high.astype(F32)
    mid = rest.astype(BF)
    low = (rest - mid.astype(F32)).astype(BF)
    terms = lax.dot_general(
        jnp.concatenate([high, mid, low], axis=0), right, (((1,), (0,)), ((), ())), preferred_element_type=F32
    ).reshape(3, 16, right.shape[1])
    return terms[0] + (terms[1] + terms[2])


def work(gate_pre, up_pre, grad_out, down_weight, basis, first_moment_in, second_moment_in):
    width = grad_out.shape[1]
    units = gate_pre.shape[1]
    core = lax.axis_index("row") % 2
    x = lax.axis_index("col") % 4

    _, _, act_early, up_early = activation(gate_pre, up_pre)
    hidden = (act_early * up_early).astype(BF)
    hidden_all = lax.all_gather(hidden, TOK, axis=0, tiled=True).reshape(32, 64, units)
    basis_all = lax.all_gather(basis, TOK, axis=0, tiled=True)
    tp_part = dot_nt(basis_all, hidden).astype(BF)
    tp_got = lax.all_to_all(tp_part, "col", 0, 0, tiled=True).reshape(32, 16, 128)
    tp_mine = jnp.sum(tp_got.astype(F32), axis=0)
    tp_all = lax.all_gather(tp_mine, TOK, axis=1, tiled=True).reshape(16, 32, 64)

    out_rows, blocks = [], []
    for begin, end in CHUNKS:
        rows = end - begin
        out = gather_rows(grad_out[begin:end], x)
        out_rows.append(out.reshape(32 * rows, width))
        part = dot_nt(out_rows[-1], down_weight).astype(BF).reshape(8, 2, 2 * rows, units)
        part_mine = lax.dynamic_index_in_dim(part, core, 1, keepdims=False).reshape(16 * rows, units)
        part_other = lax.dynamic_index_in_dim(part, 1 - core, 1, keepdims=False).reshape(16 * rows, units)
        part_got = lax.ppermute(part_other, TOK, PAIR)
        part_sum = (part_mine.astype(F32) + part_got.astype(F32)).astype(BF)
        got = lax.all_to_all(part_sum, TOK, 0, 0, tiled=True, axis_index_groups=Y_GROUPS)
        blocks.append(jnp.sum(got.reshape(8, 2, rows, units).astype(F32), axis=0).astype(BF))
    summed = jnp.concatenate(blocks, axis=1).reshape(128, units)
    gate_late, up_late, summed = lax.optimization_barrier((gate_pre, up_pre, summed))
    gate_f, sigma, act_value, up_f = activation(gate_late, up_late)
    grad_hidden = summed.astype(F32)
    grad_up = (grad_hidden * act_value).astype(BF)
    grad_gate = (grad_hidden * up_f * sigma * (1.0 + gate_f * (1.0 - sigma))).astype(BF)

    projected = sum(
        exact(tp_all[:, :, begin:end].reshape(16, -1), rows) for (begin, end), rows in zip(CHUNKS, out_rows)
    )
    first_moment = 0.9 * first_moment_in + 0.1 * projected
    second_moment = 0.999 * second_moment_in + 0.001 * projected * projected
    adapted = first_moment / first_fix / (jnp.sqrt(second_moment / second_fix) + 1e-06)
    totals = jnp.stack([jnp.sum(adapted * adapted, axis=0), jnp.sum(projected * projected, axis=0)])
    for bit in (1, 2, 4, 8, 16):
        totals = totals + lax.ppermute(totals, "col", [(c, c ^ bit) for c in range(32)])
    column_scale = jnp.sqrt(totals[0]) / (jnp.sqrt(totals[1]) + 1e-06)

    terms = [dot_tn(hidden_all[:, begin:end].reshape(-1, units), out_rows[i]) for i, (begin, end) in enumerate(CHUNKS)]
    grad_weight = sum(terms).astype(BF)
    scaled_grad = (grad_weight.astype(F32) * column_scale[None, :]).astype(BF)
    return (grad_gate, grad_up, scaled_grad, first_moment, second_moment)


def solution(mesh):
    rows = P(TOK, "col")
    cols = P("col", TOK)
    return jax.shard_map(
        work,
        mesh=mesh,
        in_specs=(rows, rows, cols, cols, rows, cols, cols),
        out_specs=(rows, rows, cols, cols, cols),
        check_vma=False,
    )
```

```python
import math

import jax
import jax.numpy as jnp
from jax import lax
from jax.experimental import pallas as pl
from jax.experimental.pallas import tpu as pltpu
from jax.sharding import PartitionSpec as P


first_fix = 1.0 - math.exp(1000.0 * math.log(0.9))
second_fix = 1.0 - math.exp(1000.0 * math.log(0.999))

BF = jnp.bfloat16
F32 = jnp.float32
TOK = ("dp", "row")
Z_GROUPS = [[4 * z + x for z in range(8)] for x in range(4)]
Y_GROUPS = [[2 * m + q for m in range(8)] for q in range(2)]
PAIR = [(k, k ^ 1) for k in range(16)]


def along_x(value, step):
    return lax.ppermute(value, "col", [(c, c - c % 4 + (c % 4 + step) % 4) for c in range(32)])


def activation(gate_pre, up_pre):
    gate_f = gate_pre.astype(F32)
    sigma = jax.nn.sigmoid(gate_f)
    return gate_f, sigma, gate_f * sigma, up_pre.astype(F32)


def dot_nt(left, right):
    return lax.dot_general(left, right, (((1,), (1,)), ((), ())), preferred_element_type=F32)


def dot_tn(left, right):
    return lax.dot_general(left, right, (((0,), (0,)), ((), ())), preferred_element_type=F32)


def along_y(value, step):
    def index(y, core):
        return 2 * (4 * (y % 2) + y // 2) + core

    return lax.ppermute(value, TOK, [(index(y, q), index((y + step) % 8, q)) for y in range(8) for q in range(2)])


def place_out_kernel(here_ref, here, left, right, far_low, far_high, own, other):
    x, core = here_ref[0], here_ref[1]
    half = far_low.shape[0]
    for back, parts in ((0, ((here, 0),)), (1, ((left, 0),)), (3, ((right, 0),)), (2, ((far_low, 0), (far_high, half)))):
        source = lax.rem(x + 4 - back, 4)
        mine = source // 2 == core
        for piece, first in parts:
            rows = pl.ds(first, piece.shape[0])

            @pl.when(mine)
            def _():
                own[rows, source % 2] = piece[...]

            @pl.when(jnp.logical_not(mine))
            def _():
                other[rows, source % 2] = piece[...]


def place_out(where, pieces):
    planes, rows, width = pieces[0].shape
    return pl.pallas_call(
        place_out_kernel,
        out_shape=[jax.ShapeDtypeStruct((planes, 2, rows, width), BF)] * 2,
        in_specs=[pl.BlockSpec(memory_space=pltpu.SMEM)] + [pl.BlockSpec(memory_space=pltpu.VMEM)] * 5,
        out_specs=[pl.BlockSpec(memory_space=pltpu.VMEM)] * 2,
        name="place_out",
    )(where, *pieces)


def place_hid_kernel(y_ref, *refs):
    pieces, out = refs[:-1], refs[-1]
    y = y_ref[0]
    half = pieces[-1].shape[0]
    for back, piece, first in (
        *((d, pieces[d], 0) for d in range(4)),
        *((8 - d, pieces[3 + d], 0) for d in range(1, 4)),
        (4, pieces[7], 0),
        (4, pieces[8], half),
    ):
        source = lax.rem(y + 8 - back, 8)
        m = 4 * (source % 2) + source // 2
        out[m, pl.ds(first, piece.shape[0])] = piece[...]


def place_hid(y, pieces):
    rows, units = pieces[0].shape
    return pl.pallas_call(
        place_hid_kernel,
        out_shape=jax.ShapeDtypeStruct((8, rows, units), BF),
        in_specs=[pl.BlockSpec(memory_space=pltpu.SMEM)] + [pl.BlockSpec(memory_space=pltpu.VMEM)] * 9,
        out_specs=pl.BlockSpec(memory_space=pltpu.VMEM),
        name="place_hid",
    )(y[None], *pieces)


def gather_out(value, where):
    sent = jnp.broadcast_to(value[None], (8,) + value.shape).reshape((-1,) + value.shape[1:])
    here = lax.all_to_all(sent, "col", 0, 0, tiled=True, axis_index_groups=Z_GROUPS)
    here = here.reshape((8,) + value.shape)
    left = along_x(here, 1)
    right = along_x(here, -1)
    far_low = along_x(left[:4], 1)
    far_high = along_x(right[4:], -1)
    return place_out(where, (here, left, right, far_low, far_high))


def gather_hid(value, y):
    up, down = [value], [value]
    for _ in range(1, 4):
        up.append(along_y(up[-1], 1))
        down.append(along_y(down[-1], -1))
    half = value.shape[0] // 2
    far_low = along_y(up[3][:half], 1)
    far_high = along_y(down[3][half:], -1)
    return place_hid(y, (*up, *down[1:], far_low, far_high))


def exact(left, right):
    high = left.astype(BF)
    rest = left - high.astype(F32)
    mid = rest.astype(BF)
    low = (rest - mid.astype(F32)).astype(BF)
    terms = lax.dot_general(
        jnp.concatenate([high, mid, low], axis=0), right, (((1,), (0,)), ((), ())), preferred_element_type=F32
    ).reshape(3, 16, right.shape[1])
    return terms[0] + (terms[1] + terms[2])


def work(gate_pre, up_pre, grad_out, down_weight, basis, first_moment_in, second_moment_in):
    width = grad_out.shape[1]
    units = gate_pre.shape[1]
    core = lax.axis_index("row") % 2
    y = 2 * (lax.axis_index("row") // 2) + lax.axis_index("dp")
    x = lax.axis_index("col") % 4

    out_own, out_other = gather_out(grad_out, jnp.stack([x, core]))
    out_own, out_other = out_own.reshape(1024, width), out_other.reshape(1024, width)

    _, _, act_early, up_early = activation(gate_pre, up_pre)
    hidden = (act_early * up_early).astype(BF)
    both = jnp.concatenate([hidden, basis], axis=0)
    both_own = gather_hid(both, y)
    both_other = lax.ppermute(both_own, TOK, PAIR)
    hidden_own, hidden_other = (v[:, :128].reshape(1024, units) for v in (both_own, both_other))

    tp_own, tp_other = (
        dot_nt(v[:, 128:].reshape(256, units), hidden).astype(BF).reshape(8, 1, 32, 128) for v in (both_own, both_other)
    )
    tp_part = jnp.where(
        core == 0,
        jnp.concatenate([tp_own, tp_other], axis=1),
        jnp.concatenate([tp_other, tp_own], axis=1),
    ).reshape(512, 128)
    tp_got = lax.all_to_all(tp_part, "col", 0, 0, tiled=True).reshape(32, 16, 128)
    tp_mine = jnp.sum(tp_got.astype(F32), axis=0)
    tp_sent = jnp.broadcast_to(tp_mine[None], (16, 16, 128)).reshape(256, 128)
    tp_all = lax.all_to_all(tp_sent, TOK, 0, 0, tiled=True).reshape(8, 2, 16, 128)

    def tp_rows(which):
        return lax.dynamic_index_in_dim(tp_all, which, 1, keepdims=False).transpose(1, 0, 2).reshape(16, 1024)

    part_other = dot_nt(out_other, down_weight).astype(BF)
    part_got = lax.ppermute(part_other, TOK, PAIR)
    part_sum = (dot_nt(out_own, down_weight) + part_got.astype(F32)).astype(BF)
    blocks = lax.all_to_all(part_sum, TOK, 0, 0, tiled=True, axis_index_groups=Y_GROUPS)
    summed = jnp.sum(blocks.reshape(8, 128, units).astype(F32), axis=0).astype(BF)
    gate_late, up_late, summed = lax.optimization_barrier((gate_pre, up_pre, summed))
    gate_f, sigma, act_value, up_f = activation(gate_late, up_late)
    grad_hidden = summed.astype(F32)
    grad_up = (grad_hidden * act_value).astype(BF)
    grad_gate = (grad_hidden * up_f * sigma * (1.0 + gate_f * (1.0 - sigma))).astype(BF)

    projected = exact(tp_rows(core), out_own) + exact(tp_rows(1 - core), out_other)
    first_moment = 0.9 * first_moment_in + 0.1 * projected
    second_moment = 0.999 * second_moment_in + 0.001 * projected * projected
    adapted = first_moment / first_fix / (jnp.sqrt(second_moment / second_fix) + 1e-06)
    totals = jnp.stack([jnp.sum(adapted * adapted, axis=0), jnp.sum(projected * projected, axis=0)])
    for bit in (1, 2, 4, 8, 16):
        totals = totals + lax.ppermute(totals, "col", [(c, c ^ bit) for c in range(32)])
    column_scale = jnp.sqrt(totals[0]) / (jnp.sqrt(totals[1]) + 1e-06)

    terms = (dot_tn(hidden_own, out_own), dot_tn(hidden_other, out_other))
    grad_weight = sum(terms).astype(BF)
    scaled_grad = (grad_weight.astype(F32) * column_scale[None, :]).astype(BF)
    return (grad_gate, grad_up, scaled_grad, first_moment, second_moment)


def solution(mesh):
    rows = P(TOK, "col")
    cols = P("col", TOK)
    return jax.shard_map(
        work,
        mesh=mesh,
        in_specs=(rows, rows, cols, cols, rows, cols, cols),
        out_specs=(rows, rows, cols, cols, cols),
        check_vma=False,
    )
```

```python
import math

import jax
import jax.numpy as jnp
from jax import lax
from jax.experimental import pallas as pl
from jax.experimental.pallas import tpu as pltpu
from jax.sharding import PartitionSpec as P


first_fix = 1.0 - math.exp(1000.0 * math.log(0.9))
second_fix = 1.0 - math.exp(1000.0 * math.log(0.999))

BF = jnp.bfloat16
F32 = jnp.float32
TOK = ("dp", "row")
Z_GROUPS = [[4 * z + x for z in range(8)] for x in range(4)]
Y_GROUPS = [[2 * m + q for m in range(8)] for q in range(2)]
PAIR = [(k, k ^ 1) for k in range(16)]


def along_x(value):
    def target(row, c):
        return row, c - c % 4 + (c + 1 - 2 * (row % 2)) % 4

    moves = [(32 * row + c, target(row, c)) for row in range(8) for c in range(32)]
    return lax.ppermute(value, ("row", "col"), [(source, 32 * row + c) for source, (row, c) in moves])


def along_y(value):
    def index(y, core):
        return 2 * (4 * (y % 2) + y // 2) + core

    return lax.ppermute(value, TOK, [(index(y, q), index((y + 1 - 2 * q) % 8, q)) for y in range(8) for q in range(2)])


def activation(gate_pre, up_pre):
    gate_f = gate_pre.astype(F32)
    sigma = jax.nn.sigmoid(gate_f)
    return gate_f, sigma, gate_f * sigma, up_pre.astype(F32)


def dot_nt(left, right):
    return lax.dot_general(left, right, (((1,), (1,)), ((), ())), preferred_element_type=F32)


def dot_tn(left, right):
    return lax.dot_general(left, right, (((0,), (0,)), ((), ())), preferred_element_type=F32)


def place_out_kernel(here_ref, *refs):
    pieces, (own, other) = refs[:-2], refs[-2:]
    x, core = here_ref[0], here_ref[1]
    for step, piece in enumerate(pieces):
        source = lax.rem(x + 4 + step * (2 * core - 1), 4)
        mine = source // 2 == core

        @pl.when(mine)
        def _():
            own[:, source % 2] = piece[...]

        @pl.when(jnp.logical_not(mine))
        def _():
            other[:, source % 2] = piece[...]


def place_out(where, pieces):
    planes, rows, width = pieces[0].shape
    return pl.pallas_call(
        place_out_kernel,
        out_shape=[jax.ShapeDtypeStruct((planes, 2, rows, width), BF)] * 2,
        in_specs=[pl.BlockSpec(memory_space=pltpu.SMEM)] + [pl.BlockSpec(memory_space=pltpu.VMEM)] * 4,
        out_specs=[pl.BlockSpec(memory_space=pltpu.VMEM)] * 2,
        name="place_out",
    )(where, *pieces)


def place_hid_kernel(here_ref, *refs):
    pieces, out = refs[:-1], refs[-1]
    y, core = here_ref[0], here_ref[1]
    for step, piece in enumerate(pieces):
        source = lax.rem(y + 8 + step * (2 * core - 1), 8)
        out[4 * (source % 2) + source // 2] = piece[...]


def place_hid(where, pieces):
    rows, units = pieces[0].shape
    return pl.pallas_call(
        place_hid_kernel,
        out_shape=jax.ShapeDtypeStruct((8, rows, units), BF),
        in_specs=[pl.BlockSpec(memory_space=pltpu.SMEM)] + [pl.BlockSpec(memory_space=pltpu.VMEM)] * 8,
        out_specs=pl.BlockSpec(memory_space=pltpu.VMEM),
        name="place_hid",
    )(where, *pieces)


def gather_out(value, where):
    sent = jnp.broadcast_to(value[None], (8,) + value.shape).reshape((-1,) + value.shape[1:])
    got = lax.all_to_all(sent, "col", 0, 0, tiled=True, axis_index_groups=Z_GROUPS)
    pieces = [got.reshape((8,) + value.shape)]
    for _ in range(1, 4):
        pieces.append(along_x(pieces[-1]))
    return place_out(where, pieces)


def gather_hid(value, where):
    pieces = [value]
    for _ in range(1, 8):
        pieces.append(along_y(pieces[-1]))
    return place_hid(where, pieces)


def exact(left, right):
    high = left.astype(BF)
    rest = left - high.astype(F32)
    mid = rest.astype(BF)
    low = (rest - mid.astype(F32)).astype(BF)
    terms = lax.dot_general(
        jnp.concatenate([high, mid, low], axis=0), right, (((1,), (0,)), ((), ())), preferred_element_type=F32
    ).reshape(3, 16, right.shape[1])
    return terms[0] + (terms[1] + terms[2])


def work(gate_pre, up_pre, grad_out, down_weight, basis, first_moment_in, second_moment_in):
    width = grad_out.shape[1]
    units = gate_pre.shape[1]
    core = lax.axis_index("row") % 2
    y = 2 * (lax.axis_index("row") // 2) + lax.axis_index("dp")
    x = lax.axis_index("col") % 4

    out_own, out_other = gather_out(grad_out, jnp.stack([x, core]))
    out_own, out_other = out_own.reshape(1024, width), out_other.reshape(1024, width)

    _, _, act_early, up_early = activation(gate_pre, up_pre)
    hidden = (act_early * up_early).astype(BF)
    hidden_own = gather_hid(hidden, jnp.stack([y, core])).reshape(1024, units)
    hidden_other = lax.ppermute(hidden_own, TOK, PAIR)

    basis_all = lax.all_gather(basis, TOK, axis=0, tiled=True)
    tp_part = dot_nt(basis_all, hidden).astype(BF)
    tp_got = lax.all_to_all(tp_part, "col", 0, 0, tiled=True).reshape(32, 16, 128)
    tp_mine = jnp.sum(tp_got.astype(F32), axis=0)
    tp_sent = jnp.broadcast_to(tp_mine[None], (16, 16, 128)).reshape(256, 128)
    tp_all = lax.all_to_all(tp_sent, TOK, 0, 0, tiled=True).reshape(8, 2, 16, 128)

    def tp_rows(which):
        return lax.dynamic_index_in_dim(tp_all, which, 1, keepdims=False).transpose(1, 0, 2).reshape(16, 1024)

    part_other = dot_nt(out_other, down_weight).astype(BF)
    part_got = lax.ppermute(part_other, TOK, PAIR)
    part_sum = (dot_nt(out_own, down_weight) + part_got.astype(F32)).astype(BF)
    blocks = lax.all_to_all(part_sum, TOK, 0, 0, tiled=True, axis_index_groups=Y_GROUPS)
    summed = jnp.sum(blocks.reshape(8, 128, units).astype(F32), axis=0).astype(BF)
    gate_late, up_late, summed = lax.optimization_barrier((gate_pre, up_pre, summed))
    gate_f, sigma, act_value, up_f = activation(gate_late, up_late)
    grad_hidden = summed.astype(F32)
    grad_up = (grad_hidden * act_value).astype(BF)
    grad_gate = (grad_hidden * up_f * sigma * (1.0 + gate_f * (1.0 - sigma))).astype(BF)

    projected = exact(tp_rows(core), out_own) + exact(tp_rows(1 - core), out_other)
    first_moment = 0.9 * first_moment_in + 0.1 * projected
    second_moment = 0.999 * second_moment_in + 0.001 * projected * projected
    adapted = first_moment / first_fix / (jnp.sqrt(second_moment / second_fix) + 1e-06)
    totals = jnp.stack([jnp.sum(adapted * adapted, axis=0), jnp.sum(projected * projected, axis=0)])
    for bit in (1, 2, 4, 8, 16):
        totals = totals + lax.ppermute(totals, "col", [(c, c ^ bit) for c in range(32)])
    column_scale = jnp.sqrt(totals[0]) / (jnp.sqrt(totals[1]) + 1e-06)

    terms = (dot_tn(hidden_own, out_own), dot_tn(hidden_other, out_other))
    grad_weight = sum(terms).astype(BF)
    scaled_grad = (grad_weight.astype(F32) * column_scale[None, :]).astype(BF)
    return (grad_gate, grad_up, scaled_grad, first_moment, second_moment)


def solution(mesh):
    rows = P(TOK, "col")
    cols = P("col", TOK)
    return jax.shard_map(
        work,
        mesh=mesh,
        in_specs=(rows, rows, cols, cols, rows, cols, cols),
        out_specs=(rows, rows, cols, cols, cols),
        check_vma=False,
    )
```

```python
import math

import jax
import jax.numpy as jnp
from jax import lax
from jax.experimental import pallas as pl
from jax.experimental.pallas import tpu as pltpu
from jax.sharding import PartitionSpec as P


first_fix = 1.0 - math.exp(1000.0 * math.log(0.9))
second_fix = 1.0 - math.exp(1000.0 * math.log(0.999))

BF = jnp.bfloat16
F32 = jnp.float32
TOK = ("dp", "row")
Z_GROUPS = [[4 * z + x for z in range(8)] for x in range(4)]
Y_GROUPS = [[2 * m + q for m in range(8)] for q in range(2)]
PAIR = [(k, k ^ 1) for k in range(16)]


def along_x(value):
    def target(row, c):
        return row, c - c % 4 + (c + 1 - 2 * (row % 2)) % 4

    moves = [(32 * row + c, target(row, c)) for row in range(8) for c in range(32)]
    return lax.ppermute(value, ("row", "col"), [(source, 32 * row + c) for source, (row, c) in moves])


def activation(gate_pre, up_pre):
    gate_f = gate_pre.astype(F32)
    sigma = jax.nn.sigmoid(gate_f)
    return gate_f, sigma, gate_f * sigma, up_pre.astype(F32)


def dot_nt(left, right):
    return lax.dot_general(left, right, (((1,), (1,)), ((), ())), preferred_element_type=F32)


def dot_tn(left, right):
    return lax.dot_general(left, right, (((0,), (0,)), ((), ())), preferred_element_type=F32)


def place_out_kernel(here_ref, *refs):
    pieces, out = refs[:-1], refs[-1]
    x, core = here_ref[0], here_ref[1]
    for step, piece in enumerate(pieces):
        out[:, lax.rem(x + 4 + step * (2 * core - 1), 4)] = piece[...]


def place_out(where, pieces):
    planes, rows, width = pieces[0].shape
    return pl.pallas_call(
        place_out_kernel,
        out_shape=jax.ShapeDtypeStruct((planes, 4, rows, width), BF),
        in_specs=[pl.BlockSpec(memory_space=pltpu.SMEM)] + [pl.BlockSpec(memory_space=pltpu.VMEM)] * 4,
        out_specs=pl.BlockSpec(memory_space=pltpu.VMEM),
        name="place_out",
    )(where, *pieces)


def gather_out(value):
    sent = jnp.broadcast_to(value[None], (8,) + value.shape).reshape((-1,) + value.shape[1:])
    got = lax.all_to_all(sent, "col", 0, 0, tiled=True, axis_index_groups=Z_GROUPS)
    pieces = [got.reshape((8,) + value.shape)]
    for _ in range(1, 4):
        pieces.append(along_x(pieces[-1]))
    return pieces


def exact(left, right):
    high = left.astype(BF)
    rest = left - high.astype(F32)
    mid = rest.astype(BF)
    low = (rest - mid.astype(F32)).astype(BF)
    terms = lax.dot_general(
        jnp.concatenate([high, mid, low], axis=0), right, (((1,), (0,)), ((), ())), preferred_element_type=F32
    ).reshape(3, 16, right.shape[1])
    return terms[0] + (terms[1] + terms[2])


def work(gate_pre, up_pre, grad_out, down_weight, basis, first_moment_in, second_moment_in):
    width = grad_out.shape[1]
    units = gate_pre.shape[1]
    core = lax.axis_index("row") % 2
    x = lax.axis_index("col") % 4
    pieces = gather_out(grad_out)

    _, _, act_early, up_early = activation(gate_pre, up_pre)
    hidden = (act_early * up_early).astype(BF)
    hidden_all = lax.all_gather(hidden, TOK, axis=0, tiled=True)

    basis_all = lax.all_gather(basis, TOK, axis=0, tiled=True)
    tp_part = dot_nt(basis_all, hidden).astype(BF)
    tp_got = lax.all_to_all(tp_part, "col", 0, 0, tiled=True).reshape(32, 16, 128)
    tp_mine = jnp.sum(tp_got.astype(F32), axis=0)
    tp_sent = jnp.broadcast_to(tp_mine[None], (16, 16, 128)).reshape(256, 128)
    tp_all = lax.all_to_all(tp_sent, TOK, 0, 0, tiled=True).reshape(16, 16, 128).transpose(1, 0, 2).reshape(16, 2048)

    parts = []
    for piece in pieces:
        parts.append(dot_nt(piece.reshape(512, width), down_weight).astype(BF))
    sums = []
    for first, second, source in ((0, 2, x), (1, 3, (x + 3 + 2 * core) % 4)):
        first_mine = source // 2 == core
        other = jnp.where(first_mine, parts[second], parts[first])
        mine = jnp.where(first_mine, parts[first], parts[second])
        got = lax.ppermute(other, TOK, PAIR)
        sums.append((mine.astype(F32) + got.astype(F32)).astype(BF).reshape(8, 64, units))
    part_sum = jnp.stack(sums, axis=1).reshape(1024, units)
    blocks = lax.all_to_all(part_sum, TOK, 0, 0, tiled=True, axis_index_groups=Y_GROUPS)
    summed = jnp.sum(blocks.reshape(8, 2, 64, units).astype(F32), axis=0).astype(BF)
    summed = jnp.where(x % 2 == 0, summed, summed[::-1]).reshape(128, units)
    gate_late, up_late, summed = lax.optimization_barrier((gate_pre, up_pre, summed))
    gate_f, sigma, act_value, up_f = activation(gate_late, up_late)
    grad_hidden = summed.astype(F32)
    grad_up = (grad_hidden * act_value).astype(BF)
    grad_gate = (grad_hidden * up_f * sigma * (1.0 + gate_f * (1.0 - sigma))).astype(BF)

    out_all = place_out(jnp.stack([x, core]), pieces).reshape(2048, width)
    projected = exact(tp_all, out_all)
    first_moment = 0.9 * first_moment_in + 0.1 * projected
    second_moment = 0.999 * second_moment_in + 0.001 * projected * projected
    adapted = first_moment / first_fix / (jnp.sqrt(second_moment / second_fix) + 1e-06)
    totals = jnp.stack([jnp.sum(adapted * adapted, axis=0), jnp.sum(projected * projected, axis=0)])
    for bit in (1, 2, 4, 8, 16):
        totals = totals + lax.ppermute(totals, "col", [(c, c ^ bit) for c in range(32)])
    column_scale = jnp.sqrt(totals[0]) / (jnp.sqrt(totals[1]) + 1e-06)

    grad_weight = dot_tn(hidden_all, out_all).astype(BF)
    scaled_grad = (grad_weight.astype(F32) * column_scale[None, :]).astype(BF)
    return (grad_gate, grad_up, scaled_grad, first_moment, second_moment)


def solution(mesh):
    rows = P(TOK, "col")
    cols = P("col", TOK)
    return jax.shard_map(
        work,
        mesh=mesh,
        in_specs=(rows, rows, cols, cols, rows, cols, cols),
        out_specs=(rows, rows, cols, cols, cols),
        check_vma=False,
    )
```

```python
import math

import jax
import jax.numpy as jnp
from jax import lax
from jax.experimental import pallas as pl
from jax.experimental.pallas import tpu as pltpu
from jax.sharding import PartitionSpec as P


first_fix = 1.0 - math.exp(1000.0 * math.log(0.9))
second_fix = 1.0 - math.exp(1000.0 * math.log(0.999))

BF = jnp.bfloat16
F32 = jnp.float32
TOK = ("dp", "row")
Z_GROUPS = [[4 * z + x for z in range(8)] for x in range(4)]
Y_GROUPS = [[2 * m + q for m in range(8)] for q in range(2)]
PAIR = [(k, k ^ 1) for k in range(16)]


def along_x(value):
    def target(row, c):
        return row, c - c % 4 + (c + 1 - 2 * (row % 2)) % 4

    moves = [(32 * row + c, target(row, c)) for row in range(8) for c in range(32)]
    return lax.ppermute(value, ("row", "col"), [(source, 32 * row + c) for source, (row, c) in moves])


def along_y(value):
    def index(y, core):
        return 2 * (4 * (y % 2) + y // 2) + core

    return lax.ppermute(value, TOK, [(index(y, q), index((y + 1 - 2 * q) % 8, q)) for y in range(8) for q in range(2)])


def activation(gate_pre, up_pre):
    gate_f = gate_pre.astype(F32)
    sigma = jax.nn.sigmoid(gate_f)
    return gate_f, sigma, gate_f * sigma, up_pre.astype(F32)


def dot_nt(left, right):
    return lax.dot_general(left, right, (((1,), (1,)), ((), ())), preferred_element_type=F32)


def dot_tn(left, right):
    return lax.dot_general(left, right, (((0,), (0,)), ((), ())), preferred_element_type=F32)


def place_out_kernel(here_ref, *refs):
    pieces, (own, other) = refs[:-2], refs[-2:]
    x, core = here_ref[0], here_ref[1]
    for step, piece in enumerate(pieces):
        source = lax.rem(x + 4 + step * (2 * core - 1), 4)
        mine = source // 2 == core

        @pl.when(mine)
        def _():
            own[:, source % 2] = piece[...]

        @pl.when(jnp.logical_not(mine))
        def _():
            other[:, source % 2] = piece[...]


def place_out(where, pieces):
    planes, rows, width = pieces[0].shape
    return pl.pallas_call(
        place_out_kernel,
        out_shape=[jax.ShapeDtypeStruct((planes, 2, rows, width), BF)] * 2,
        in_specs=[pl.BlockSpec(memory_space=pltpu.SMEM)] + [pl.BlockSpec(memory_space=pltpu.VMEM)] * 4,
        out_specs=[pl.BlockSpec(memory_space=pltpu.VMEM)] * 2,
        name="place_out",
    )(where, *pieces)


def place_hid_kernel(here_ref, *refs):
    pieces, out = refs[:-1], refs[-1]
    y, core = here_ref[0], here_ref[1]
    for step, piece in enumerate(pieces):
        source = lax.rem(y + 8 + step * (2 * core - 1), 8)
        out[4 * (source % 2) + source // 2] = piece[...]


def place_hid(where, pieces):
    rows, units = pieces[0].shape
    return pl.pallas_call(
        place_hid_kernel,
        out_shape=jax.ShapeDtypeStruct((8, rows, units), BF),
        in_specs=[pl.BlockSpec(memory_space=pltpu.SMEM)] + [pl.BlockSpec(memory_space=pltpu.VMEM)] * 8,
        out_specs=pl.BlockSpec(memory_space=pltpu.VMEM),
        name="place_hid",
    )(where, *pieces)


def gather_out(value):
    sent = jnp.broadcast_to(value[None], (8,) + value.shape).reshape((-1,) + value.shape[1:])
    got = lax.all_to_all(sent, "col", 0, 0, tiled=True, axis_index_groups=Z_GROUPS)
    pieces = [got.reshape((8,) + value.shape)]
    for _ in range(1, 4):
        pieces.append(along_x(pieces[-1]))
    return pieces


def gather_hid(value, where):
    pieces = [value]
    for _ in range(1, 8):
        pieces.append(along_y(pieces[-1]))
    return place_hid(where, pieces)


def exact(left, right):
    high = left.astype(BF)
    rest = left - high.astype(F32)
    mid = rest.astype(BF)
    low = (rest - mid.astype(F32)).astype(BF)
    terms = lax.dot_general(
        jnp.concatenate([high, mid, low], axis=0), right, (((1,), (0,)), ((), ())), preferred_element_type=F32
    ).reshape(3, 16, right.shape[1])
    return terms[0] + (terms[1] + terms[2])


def work(gate_pre, up_pre, grad_out, down_weight, basis, first_moment_in, second_moment_in):
    width = grad_out.shape[1]
    units = gate_pre.shape[1]
    core = lax.axis_index("row") % 2
    y = 2 * (lax.axis_index("row") // 2) + lax.axis_index("dp")
    x = lax.axis_index("col") % 4
    pieces = gather_out(grad_out)

    _, _, act_early, up_early = activation(gate_pre, up_pre)
    hidden = (act_early * up_early).astype(BF)
    hidden_own = gather_hid(hidden, jnp.stack([y, core])).reshape(1024, units)
    hidden_other = lax.ppermute(hidden_own, TOK, PAIR)

    basis_all = lax.all_gather(basis, TOK, axis=0, tiled=True)
    tp_part = dot_nt(basis_all, hidden).astype(BF)
    tp_got = lax.all_to_all(tp_part, "col", 0, 0, tiled=True).reshape(32, 16, 128)
    tp_mine = jnp.sum(tp_got.astype(F32), axis=0)
    tp_sent = jnp.broadcast_to(tp_mine[None], (16, 16, 128)).reshape(256, 128)
    tp_all = lax.all_to_all(tp_sent, TOK, 0, 0, tiled=True).reshape(8, 2, 16, 128)

    def tp_rows(which):
        return lax.dynamic_index_in_dim(tp_all, which, 1, keepdims=False).transpose(1, 0, 2).reshape(16, 1024)

    parts = []
    for piece in pieces:
        parts.append(dot_nt(piece.reshape(512, width), down_weight).astype(BF))
    sums = []
    for first, second, source in ((0, 2, x), (1, 3, (x + 3 + 2 * core) % 4)):
        first_mine = source // 2 == core
        other = jnp.where(first_mine, parts[second], parts[first])
        mine = jnp.where(first_mine, parts[first], parts[second])
        got = lax.ppermute(other, TOK, PAIR)
        sums.append((mine.astype(F32) + got.astype(F32)).astype(BF).reshape(8, 64, units))
    part_sum = jnp.stack(sums, axis=1).reshape(1024, units)
    blocks = lax.all_to_all(part_sum, TOK, 0, 0, tiled=True, axis_index_groups=Y_GROUPS)
    summed = jnp.sum(blocks.reshape(8, 2, 64, units).astype(F32), axis=0).astype(BF)
    summed = jnp.where(x % 2 == 0, summed, summed[::-1]).reshape(128, units)
    gate_late, up_late, summed = lax.optimization_barrier((gate_pre, up_pre, summed))
    gate_f, sigma, act_value, up_f = activation(gate_late, up_late)
    grad_hidden = summed.astype(F32)
    grad_up = (grad_hidden * act_value).astype(BF)
    grad_gate = (grad_hidden * up_f * sigma * (1.0 + gate_f * (1.0 - sigma))).astype(BF)

    out_own, out_other = place_out(jnp.stack([x, core]), pieces)
    out_own, out_other = out_own.reshape(1024, width), out_other.reshape(1024, width)
    projected = exact(tp_rows(core), out_own) + exact(tp_rows(1 - core), out_other)
    first_moment = 0.9 * first_moment_in + 0.1 * projected
    second_moment = 0.999 * second_moment_in + 0.001 * projected * projected
    adapted = first_moment / first_fix / (jnp.sqrt(second_moment / second_fix) + 1e-06)
    totals = jnp.stack([jnp.sum(adapted * adapted, axis=0), jnp.sum(projected * projected, axis=0)])
    for bit in (1, 2, 4, 8, 16):
        totals = totals + lax.ppermute(totals, "col", [(c, c ^ bit) for c in range(32)])
    column_scale = jnp.sqrt(totals[0]) / (jnp.sqrt(totals[1]) + 1e-06)

    terms = (dot_tn(hidden_own, out_own), dot_tn(hidden_other, out_other))
    grad_weight = sum(terms).astype(BF)
    scaled_grad = (grad_weight.astype(F32) * column_scale[None, :]).astype(BF)
    return (grad_gate, grad_up, scaled_grad, first_moment, second_moment)


def solution(mesh):
    rows = P(TOK, "col")
    cols = P("col", TOK)
    return jax.shard_map(
        work,
        mesh=mesh,
        in_specs=(rows, rows, cols, cols, rows, cols, cols),
        out_specs=(rows, rows, cols, cols, cols),
        check_vma=False,
    )
```
